512 devices in a mesh: head: 8 (over z), blk: 64 (over x, y, core).
Axes of the slice: x: 4, y: 8, z: 8, core: 2. Of those that a mesh axis runs over, the one named last changes fastest.
Arguments:
- vision: bfloat16 [4, 1408, 8192], P(None, 'head', 'blk'), may hold values from -600 to 600
- ln_gain: float32 [1408], P('head'), may hold values from 0.5 to 1.5
- merge_proj: bfloat16 [4, 1408, 1408], P(None, 'head'), may hold values from -0.078125 to 0.078125
- image_slot: int32 [2048], P('blk'), may hold values from 0 to 32764, as said below
- text: bfloat16 [1408, 32768], P('head', 'blk'), may hold values from -600 to 600
- rms_gain: float32 [1408], replicated, may hold values from 0.5 to 1.5
- wqkv: bfloat16 [3, 1408, 1408], P(None, 'head'), may hold values from -0.31835938 to 0.31835938
- pcache: bfloat16 [2, 1408, 131072], P(None, 'head', 'blk'), may hold values from -300 to 300
- block_table: int32 [64, 128], replicated, may hold values from -1 to 4095, as said below
- cache_len: int32 [64], P('blk'), may hold values from 1 to 4096, as said below
Outputs:
- attended: bfloat16 [1408, 32768], P('head', 'blk')
- new_cache: bfloat16 [2, 1408, 32768], P(None, 'head', 'blk')
The draws below stay inside these ranges and needn't reach their ends.
Inputs may be any that keep to these rules, and one draw needn't show every extreme that they name: `image_slot`: pieces never intersect and start at multiples of 4; the 32 pieces held by one index of blk start in the rows of 32 different requests, and every request receives exactly 32 pieces. `block_table`: row r holds a block number for j < ceil(cache_len[r] / 32) and -1 after; no block number appears twice; index d of blk holds blocks d * 64 to (d+1) * 64 - 1. The longest request has exactly 2 blocks on every index of blk; every other request has at most one block on any index. `cache_len`: exactly one request, the longest, has 4096 cached positions; all others have fewer.
All inputs are finite; a program needn't handle non-finite values.
Results may differ from the reference program's by a relative error of at most 0.025.
The reference program's roundings to bfloat16 on the way count: a program that leaves them out, or rounds other values in their place, can miss the bound.
Values may be sent and summed in bfloat16 or wider, within the bound.
A program may use at most 128 MiB of HBM per device.

```python
import math
import jax
import jax.numpy as jnp
from jax import lax

D = 1408
HD = 88
PIECE = 4
BS = 32
PT_DEV = 512
BLK_DEV = 64
IMG_DEV = 32
VT = 32768
REQS = 64
NEW = 32768
MAXB = 128
TOTB = 3152
NPHYS = 4096


def scaled_rows(key, rows):
    keys = jax.random.split(key, 3)
    columns = jnp.exp(jnp.arange(D, dtype=jnp.float32) * (math.log(3.0) / D))
    columns = columns * jnp.exp(math.log(3.3) * jax.random.uniform(keys[1], (D,), dtype=jnp.float32))
    row_scale = jnp.exp(math.log(10.0) * jax.random.uniform(keys[2], (rows, 1), dtype=jnp.float32))
    base = jax.random.normal(keys[0], (rows, D), dtype=jnp.float32)
    return (jnp.clip(base, -5.0, 5.0) * columns * row_scale).astype(jnp.bfloat16)


def draw_vision(key, part):
    rows = scaled_rows(jax.random.fold_in(key, 3), VT)
    return jnp.transpose(rows.reshape(VT // 4, 4, D), (1, 2, 0))


def draw_text(key, part):
    return jnp.transpose(scaled_rows(jax.random.fold_in(key, 5), NEW))


def draw_pcache(key, part):
    keys = jax.random.split(jax.random.fold_in(key, 7), 1)
    shape = (NPHYS, BS, 2, D)
    base = jnp.clip(2.0 * jax.random.normal(keys[0], shape, dtype=jnp.float32), -12.0, 12.0)
    return jnp.transpose(base.astype(jnp.bfloat16), (2, 3, 0, 1)).reshape(2, D, NPHYS * BS)


def draw_image_slot(key, part):
    keys = jax.random.split(jax.random.fold_in(key, 11), 4)
    count = REQS
    shuffle_a = jax.random.permutation(keys[0], count)
    shuffle_b = jax.random.permutation(keys[1], count)
    shifts = jax.random.permutation(keys[2], count)[:IMG_DEV]
    target = shuffle_b[(shuffle_a[:, None] + shifts[None, :]) % count]
    slots = PT_DEV // PIECE

    def order_for(device):
        return jax.random.permutation(jax.random.fold_in(keys[3], device), slots)[:IMG_DEV]
    orders = jax.vmap(order_for)(jnp.arange(count))
    chosen = orders[target, jnp.arange(IMG_DEV)[None, :]]
    return (target * PT_DEV + chosen * PIECE).reshape(-1).astype(jnp.int32)


def block_plan(key):
    keys = jax.random.split(jax.random.fold_in(key, 29), 5)
    count = REQS
    idents = jnp.arange(count)
    longest = jax.random.randint(keys[0], (), 0, count)
    others = idents != longest
    shares = jnp.where(others, jax.random.randint(keys[1], (count,), 4, 6), 0)
    spare_blocks = TOTB - MAXB - (count - 1)
    extra = spare_blocks * shares // jnp.sum(shares)
    leftover = spare_blocks - jnp.sum(extra)
    standing = jnp.cumsum(others.astype(jnp.int32)) - 1
    extra = extra + jnp.where(others & (standing < leftover), 1, 0)
    nblocks = jnp.where(others, 1 + extra, MAXB)
    tails = jax.random.randint(keys[2], (count,), 1, BS + 1)
    lengths = (nblocks - 1) * BS + jnp.where(others, tails, BS)
    begins = jnp.cumsum(nblocks) - nblocks
    shuffle_dev = jax.random.permutation(keys[3], count)

    def slots_for(device):
        return jax.random.permutation(jax.random.fold_in(keys[4], device), BLK_DEV)
    local_slots = jax.vmap(slots_for)(idents)
    columns = jnp.arange(MAXB)
    running = begins[:, None] + columns[None, :]
    device = shuffle_dev[running % count]
    layer = jnp.minimum(running // count, BLK_DEV - 1)
    physical = device * BLK_DEV + local_slots[device, layer]
    table = jnp.where(columns[None, :] < nblocks[:, None], physical, -1)
    return (table.astype(jnp.int32), lengths.astype(jnp.int32))


def draw_block_table(key, part):
    return block_plan(key)[0]


def draw_cache_len(key, part):
    return block_plan(key)[1]


def steps_of(own_key, extent, cuts, least, high):
    level, own = 1.0, jax.random.fold_in(own_key, 6)
    for position, shards_of in cuts:
        steps = jnp.exp(jax.random.uniform(jax.random.fold_in(own, position), (shards_of,), jnp.float32, least / len(cuts), high / len(cuts)))
        level = level * jnp.repeat(steps, extent[position] // shards_of).reshape([-1 if axis == position else 1 for axis in range(len(extent))])
    return level


def noise(key, dims, deviation, most, cuts=(), kind=jnp.bfloat16):
    entries = jax.random.normal(key, dims, jnp.float32) * deviation
    if len(cuts) > 0:
        entries = steps_of(key, dims, cuts, -0.22, 0.18) * entries
    return jnp.clip(entries, min=-most, max=most).astype(kind)


def setup_inputs(seed: int = 0) -> dict:
    streams_of = jax.random.split(jax.random.key(seed), 11)
    vision = draw_vision(jax.random.fold_in(streams_of[10], 71), 0)
    ln_gain = jnp.clip(1.0 + 0.1 * jax.random.normal(streams_of[1], (D,), jnp.float32), 0.5, 1.5)
    merge_proj = noise(streams_of[2], (4, D, D), (4 * D) ** -0.5, 0.078125, ((1, 8),))
    image_slot = draw_image_slot(jax.random.fold_in(streams_of[10], 71), 0)
    text = draw_text(jax.random.fold_in(streams_of[10], 71), 0)
    rms_gain = jnp.clip(1.0 + 0.1 * jax.random.normal(streams_of[5], (D,), jnp.float32), 0.5, 1.5)
    wqkv = noise(streams_of[6], (3, D, D), 0.0533, 0.31835938, ((1, 8),))
    pcache = draw_pcache(jax.random.fold_in(streams_of[10], 71), 0)
    block_table = draw_block_table(jax.random.fold_in(streams_of[10], 71), 0)
    cache_len = draw_cache_len(jax.random.fold_in(streams_of[10], 71), 0)
    return {"vision": vision, "ln_gain": ln_gain, "merge_proj": merge_proj, "image_slot": image_slot, "text": text, "rms_gain": rms_gain, "wqkv": wqkv, "pcache": pcache, "block_table": block_table, "cache_len": cache_len}


masked_score = -1e+30

def rotary(values, places):
    half = values.shape[-1] // 2
    freq_index = jnp.arange(half, dtype=jnp.float32)
    inverse = jnp.exp(freq_index * (-2.0 * math.log(10000.0) / values.shape[-1]))
    angles = places[:, None] * inverse[None, :]
    cosine = jnp.cos(angles)[:, None, :]
    sine_part = jnp.sin(angles)[:, None, :]
    leading = values[..., :half]
    trailing = values[..., half:]
    return jnp.concatenate([leading * cosine - trailing * sine_part, trailing * cosine + leading * sine_part], axis=-1)

def reference(vision, ln_gain, merge_proj, image_slot, text, rms_gain, wqkv, pcache, block_table, cache_len):
    width = vision.shape[1]
    groups = vision.shape[2]
    vision_rows = jnp.transpose(vision, (2, 0, 1)).reshape(groups * 4, width)
    text_rows = jnp.transpose(text)
    weight_rows = jnp.transpose(wqkv, (2, 0, 1))
    floats = vision_rows.astype(jnp.float32)
    average = lax.optimization_barrier(jnp.sum(floats, axis=1)) / width
    spread = lax.optimization_barrier(jnp.sum(floats * floats, axis=1)) / width - average * average
    normed_vision = ((floats - average[:, None]) * lax.rsqrt(spread + 1e-06)[:, None] * ln_gain).astype(jnp.bfloat16)
    merged = jnp.dot(normed_vision.reshape(groups, 4 * width), merge_proj.reshape(4 * width, width), preferred_element_type=jnp.float32).astype(jnp.bfloat16)
    piece_rows = groups // image_slot.shape[0]
    targets = (image_slot[:, None] + jnp.arange(piece_rows, dtype=jnp.int32)[None, :]).reshape(-1).astype(jnp.int32)
    placed = text_rows.at[targets].set(merged)
    row_floats = placed.astype(jnp.float32)
    mean_square = lax.optimization_barrier(jnp.sum(row_floats * row_floats, axis=1)) / width
    normed = (row_floats * lax.rsqrt(mean_square + 1e-06)[:, None] * rms_gain).astype(jnp.bfloat16)
    projected = jnp.dot(normed, weight_rows.reshape(width, 3 * width), preferred_element_type=jnp.float32)
    total_rows = text_rows.shape[0]
    requests = cache_len.shape[0]
    per_request = total_rows // requests
    head_size = HD
    heads = width // head_size
    projected = projected.reshape(total_rows, 3, heads, head_size)
    places = (jnp.repeat(cache_len, per_request) + jnp.tile(jnp.arange(per_request, dtype=jnp.int32), requests)).astype(jnp.float32)
    queries = rotary(projected[:, 0], places).astype(jnp.bfloat16)
    new_keys = rotary(projected[:, 1], places).astype(jnp.bfloat16)
    new_values = projected[:, 2].astype(jnp.bfloat16)
    new_cache = jnp.stack([new_keys.reshape(total_rows, width), new_values.reshape(total_rows, width)], axis=1)
    block_len = BS
    physical = pcache.shape[2] // block_len
    paged = pcache.reshape(2, width, physical, block_len)
    table_width = block_table.shape[1]
    scale = head_size ** (-0.5)
    lines = jnp.arange(per_request, dtype=jnp.int32)
    causal = lines[:, None] >= lines[None, :]

    def one_request(inputs):
        query_rows, key_rows, value_rows, table_row, length = inputs
        blocks = paged[:, :, jnp.clip(table_row, 0, physical - 1).astype(jnp.int32), :]
        cached_keys = jnp.transpose(blocks[0].reshape(width, table_width * block_len)).reshape(table_width * block_len, heads, head_size).astype(jnp.float32)
        cached_values = jnp.transpose(blocks[1].reshape(width, table_width * block_len)).reshape(table_width * block_len, heads, head_size).astype(jnp.float32)
        live = jnp.arange(table_width * block_len, dtype=jnp.int32) < length
        query_floats = query_rows.astype(jnp.float32)
        old_scores = jnp.einsum('qhd,khd->hqk', query_floats, cached_keys) * scale
        own_scores = jnp.einsum('qhd,khd->hqk', query_floats, key_rows.astype(jnp.float32)) * scale
        old_scores = jnp.where(live[None, None, :], old_scores, masked_score)
        own_scores = jnp.where(causal[None], own_scores, masked_score)
        highest = jnp.maximum(lax.optimization_barrier(jnp.max(old_scores, axis=2)), lax.optimization_barrier(jnp.max(own_scores, axis=2)))
        old_exp = jnp.exp(old_scores - highest[:, :, None])
        own_exp = jnp.exp(own_scores - highest[:, :, None])
        total = lax.optimization_barrier(jnp.sum(old_exp, axis=2)) + lax.optimization_barrier(jnp.sum(own_exp, axis=2))
        old_weights = old_exp / total[:, :, None]
        own_weights = own_exp / total[:, :, None]
        mixed = jnp.einsum('hqk,khd->qhd', old_weights, cached_values, precision=lax.Precision.HIGHEST)
        mixed = mixed + jnp.einsum('hqk,khd->qhd', own_weights, value_rows.astype(jnp.float32), precision=lax.Precision.HIGHEST)
        return mixed.astype(jnp.bfloat16).reshape(per_request, width)
    attended = lax.map(one_request, (queries.reshape(requests, per_request, heads, head_size), new_keys.reshape(requests, per_request, heads, head_size), new_values.reshape(requests, per_request, heads, head_size), block_table, cache_len)).reshape(total_rows, width)
    return (jnp.transpose(attended), jnp.transpose(new_cache, (1, 2, 0)))
```

```python
import functools
import math

import jax
import jax.numpy as jnp
from jax import lax
from jax.experimental import pallas as pl
from jax.experimental.pallas import tpu as pltpu
from jax.sharding import PartitionSpec as P

HD = 88
BS = 32
MESH = pl.DeviceIdType.MESH
GRID = {64: (4, 8, 2), 8: (2, 2, 2)}
F32 = jnp.float32
BF16 = jnp.bfloat16
NEG = -1e30


def dot(a, b, ca=1, cb=0):
    return lax.dot_general(a, b, (((ca,), (cb,)), ((), ())), preferred_element_type=F32)


def iota(shape, dim):
    return lax.broadcasted_iota(jnp.int32, shape, dim)


def comm_kernel(
    width,
    rows_here,
    idx_ref,
    image_slot_ref,
    gain_ref,
    vision_hbm,
    proj_hbm,
    pcache_hbm,
    slots_out,
    extra_out,
    img_out,
    meta_out,
    vision,
    proj,
    pcache,
    staged,
    outgoing,
    stats,
    stats_in,
    parts,
    parts_in,
    pieces,
    pieces_in,
    img,
    load_sem,
    local_sem,
    send_sem,
    recv_sem,
):
    z = lax.axis_index("head")
    me = lax.axis_index("blk")
    zs = stats_in.shape[0]
    devices = slots_out.shape[0]
    cs, xs, ys = extra_out.shape[:3]
    my_c = lax.rem(me, cs)
    my_y = lax.rem(me // cs, ys)
    my_x = me // (cs * ys)
    local = vision.shape[1]
    groups = vision.shape[2]

    load_vision = pltpu.make_async_copy(vision_hbm, vision, load_sem.at[0])
    load_pcache = pltpu.make_async_copy(pcache_hbm, pcache, load_sem.at[1])
    load_proj = pltpu.make_async_copy(proj_hbm, proj, load_sem.at[2])
    load_vision.start()
    load_pcache.start()
    load_proj.start()

    barrier = pltpu.get_barrier_semaphore()

    @pl.loop(1, devices)
    def _(step):
        pl.semaphore_signal(
            barrier, inc=1, device_id=(z, lax.rem(me + step, devices)), device_id_type=MESH
        )

    @pl.loop(1, zs)
    def _(step):
        pl.semaphore_signal(
            barrier, inc=1, device_id=(lax.rem(z + step, zs), me), device_id_type=MESH
        )

    def send(src, dst, phase, device):
        return pltpu.make_async_remote_copy(
            src_ref=src,
            dst_ref=dst,
            send_sem=send_sem.at[phase],
            recv_sem=recv_sem.at[phase],
            device_id=device,
            device_id_type=MESH,
        )

    def over_z(src_of, dst, phase):
        @pl.loop(1, zs)
        def _(step):
            other = lax.rem(z + step, zs)
            send(src_of(other), dst, phase, (other, me)).start()

    def await_in(ref, phase):
        send(ref, ref, phase, (z, me)).wait_recv()

    def await_out(ref, phase):
        send(ref, ref, phase, (z, me)).wait_send()

    load_vision.wait()
    sums, squares = [], []
    for t in range(4):
        rows = vision[t].astype(F32)
        sums.append(jnp.sum(rows, axis=0, keepdims=True))
        squares.append(jnp.sum(rows * rows, axis=0, keepdims=True))
    stats[...] = jnp.concatenate(sums + squares, axis=0)
    stats_in[pl.ds(z, 1)] = stats[...][None]
    pl.semaphore_wait(barrier, devices - 1 + zs - 1)
    over_z(lambda other: stats, stats_in.at[z], 0)

    load_pcache.wait()

    @pl.loop(0, pcache.shape[2] // 128)
    def _(column):
        lanes = pl.ds(pl.multiple_of(column * 128, 128), 128)
        tiles = [pcache[j, :, lanes] for j in range(4)]
        for o in range(4):
            staged[column * 4 + o] = jnp.concatenate(
                [tile[:, o * BS : (o + 1) * BS] for tile in tiles], axis=1
            )

    outgoing[devices] = staged[idx_ref[devices]]
    own_extra = pltpu.make_async_copy(
        outgoing.at[devices], extra_out.at[my_c, my_x, my_y], local_sem.at[0]
    )
    own_extra.start()

    @pl.loop(1, ys)
    def _(step):
        other = (my_x * ys + lax.rem(my_y + step, ys)) * cs + my_c
        send(outgoing.at[devices], extra_out.at[my_c, my_x, my_y], 4, (z, other)).start()

    @pl.loop(1, devices)
    def _(step):
        other = lax.rem(me + step, devices)
        outgoing[other] = staged[idx_ref[other]]
        send(outgoing.at[other], slots_out.at[me], 1, (z, other)).start()

    outgoing[me] = staged[idx_ref[me]]
    own_slot = pltpu.make_async_copy(outgoing.at[me], slots_out.at[me], local_sem.at[1])
    own_slot.start()

    square = iota((local, local), 0) == iota((local, local), 1)
    gain = jnp.sum(jnp.where(square, gain_ref[...], 0.0), axis=1, keepdims=True)
    load_proj.wait()
    await_in(stats_in.at[pl.ds(0, zs - 1)], 0)
    total = jnp.sum(stats_in[...], axis=0) / width
    average = total[0:4]
    scale = lax.rsqrt(total[4:8] - average * average + 1e-06)
    normed = jnp.concatenate(
        [
            (vision[t].astype(F32) - average[t : t + 1]) * scale[t : t + 1] * gain
            for t in range(4)
        ],
        axis=0,
    ).astype(BF16)
    partial_rows = dot(normed, proj[...], 0, 0)
    partial_columns = jnp.transpose(partial_rows)
    parts[...] = partial_columns.astype(BF16).reshape(parts.shape)
    parts_in[pl.ds(z, 1)] = parts[pl.ds(z, 1)]
    over_z(lambda other: parts.at[other], parts_in.at[z], 2)

    own_extra.wait()
    await_in(extra_out.at[0, 0, pl.ds(0, ys - 1)], 4)

    @pl.loop(1, xs)
    def _(step):
        other = (lax.rem(my_x + step, xs) * ys + my_y) * cs + my_c
        send(extra_out.at[my_c, my_x], extra_out.at[my_c, my_x], 5, (z, other)).start()

    count = image_slot_ref.shape[1]
    spread = (iota((count, groups), 1) // 4 == iota((count, groups), 0)).astype(BF16)
    slot = image_slot_ref[...]
    target = dot((slot // rows_here).astype(F32).astype(BF16), spread)
    place = dot((lax.rem(slot, rows_here) // 4 + 1).astype(F32).astype(BF16), spread)
    diagonal = iota((groups, groups), 0) == iota((groups, groups), 1)
    place_column = jnp.sum(jnp.where(diagonal, place, 0.0), axis=1, keepdims=True)
    line = iota((devices * 8, 2 * groups), 0)
    column = iota((devices * 8, 2 * groups), 1)
    wanted = jnp.concatenate([target, target], axis=1).astype(jnp.int32)
    half = (column >= groups).astype(jnp.int32) * 4
    select = ((line // 8) == wanted) & (lax.rem(line, 8) == (lax.rem(column, 4) + half))
    await_in(parts_in.at[pl.ds(0, zs - 1)], 2)
    merged = jnp.sum(parts_in[...].astype(F32), axis=0)
    high = jnp.concatenate(
        [merged[128:], jnp.zeros((256 - local, groups), F32)], axis=0
    )
    merged_rows = jnp.transpose(merged[:128])
    high_rows = jnp.transpose(high)
    high_rows = jnp.where(iota((groups, 128), 1) == local - 128, place_column, high_rows)
    both = jnp.concatenate([merged_rows, high_rows], axis=0).astype(BF16)
    pieces[...] = dot(select.astype(F32).astype(BF16), both).astype(BF16).reshape(pieces.shape)
    pieces_in[pl.ds(me, 1)] = pieces[pl.ds(me, 1)]

    @pl.loop(1, devices)
    def _(step):
        other = lax.rem(me + step, devices)
        send(pieces.at[other], pieces_in.at[me], 3, (z, other)).start()

    await_in(extra_out.at[0, pl.ds(0, xs - 1)], 5)
    last = send(
        extra_out.at[my_c], extra_out.at[my_c], 6, (z, (my_x * ys + my_y) * cs + (cs - 1 - my_c))
    )
    last.start()

    span = devices * 8
    earlier = (iota((span, span), 0) // 8 < iota((span, span), 1) // 8) & (
        lax.rem(iota((span, span), 0), 8) == 4
    )
    same = (iota((span, span), 0) // 8 == iota((span, span), 1) // 8) & (
        lax.rem(iota((span, span), 0), 8) == 4
    )
    earlier = earlier.astype(F32).astype(BF16)
    same = same.astype(F32).astype(BF16)
    await_in(pieces_in.at[pl.ds(0, devices - 1)], 3)
    arrived = jnp.transpose(pieces_in[...].reshape(span, 128).astype(F32)).astype(BF16)
    marks = jnp.broadcast_to(arrived[local - 128 : local - 127].astype(F32), (8, span))
    present = (marks > 0.0).astype(F32)
    rank = dot(present.astype(BF16), earlier)[0:1]
    mark = dot(marks.astype(BF16), same)
    within = lax.rem(iota((groups, span), 1), 8)
    order = jnp.where(mark[0:1] > 0.0, rank, -1.0).astype(jnp.int32) * 4
    first = (within < 4) & (iota((groups, span), 0) == order + within)
    second = (within >= 4) & (iota((groups, span), 0) == order + within - 4)
    first = first.astype(F32).astype(BF16)
    second = second.astype(F32).astype(BF16)
    low = dot(arrived, first, 1, 1)
    high = dot(arrived, second, 1, 1)
    img[...] = jnp.concatenate([low, high[: local - 128]], axis=0).astype(BF16)
    meta_out[...] = dot(mark.astype(BF16), first, 1, 1)
    own_img = pltpu.make_async_copy(img, img_out.at[z], local_sem.at[2])
    own_img.start()
    over_z(lambda other: img, img_out.at[z], 7)

    await_in(img_out.at[pl.ds(0, zs - 1)], 7)
    await_in(slots_out.at[pl.ds(0, devices - 1)], 1)
    last.wait_recv()
    own_slot.wait()
    own_img.wait()
    await_out(stats_in.at[pl.ds(0, zs - 1)], 0)
    await_out(slots_out.at[pl.ds(0, devices - 1)], 1)
    await_out(parts_in.at[pl.ds(0, zs - 1)], 2)
    await_out(pieces_in.at[pl.ds(0, devices - 1)], 3)
    await_out(extra_out.at[0, 0, pl.ds(0, ys - 1)], 4)
    await_out(extra_out.at[0, pl.ds(0, xs - 1)], 5)
    last.wait_send()
    await_out(img_out.at[pl.ds(0, zs - 1)], 7)


def communicate(width, rows, indices, image_slot, ln_gain, vision, merge_proj, pcache, devices, zs):
    xs, ys, cs = GRID[devices]
    _, local, groups = vision.shape
    vmem = pltpu.VMEM
    anywhere = pl.BlockSpec(memory_space=pl.ANY)
    inside = pl.BlockSpec(memory_space=pltpu.VMEM)
    tile = (HD, 4 * BS)
    blocks = pcache.shape[2] // BS
    return pl.pallas_call(
        functools.partial(comm_kernel, width, rows),
        out_shape=(
            jax.ShapeDtypeStruct((devices,) + tile, BF16),
            jax.ShapeDtypeStruct((cs, xs, ys) + tile, BF16),
            jax.ShapeDtypeStruct((zs, local, groups), BF16),
            jax.ShapeDtypeStruct((8, groups), F32),
        ),
        in_specs=[pl.BlockSpec(memory_space=pltpu.SMEM), inside, inside, anywhere, anywhere, anywhere],
        out_specs=(anywhere, anywhere, anywhere, inside),
        scratch_shapes=[
            vmem(vision.shape, BF16),
            vmem(merge_proj.shape, BF16),
            vmem(pcache.shape, BF16),
            vmem((blocks,) + tile, BF16),
            vmem((devices + 1,) + tile, BF16),
            vmem((8, groups), F32),
            vmem((zs, 8, groups), F32),
            vmem((zs, local, groups), BF16),
            vmem((zs, local, groups), BF16),
            vmem((devices, 8, 128), BF16),
            vmem((devices, 8, 128), BF16),
            vmem((local, groups), BF16),
            pltpu.SemaphoreType.DMA((3,)),
            pltpu.SemaphoreType.DMA((3,)),
            pltpu.SemaphoreType.DMA((8,)),
            pltpu.SemaphoreType.DMA((8,)),
        ],
        compiler_params=pltpu.CompilerParams(
            collective_id=0, has_side_effects=True, vmem_limit_bytes=48 << 20
        ),
        name="exchange",
    )(indices, image_slot, ln_gain, vision, merge_proj, pcache)


def attend_kernel(
    grid,
    counts_ref,
    text_ref,
    img_ref,
    meta_ref,
    gain_ref,
    weight_ref,
    cosine_ref,
    sine_ref,
    slots_ref,
    extra_hbm,
    attended_ref,
    cache_ref,
    extra,
    keys,
    values,
    scores,
    normed_ref,
    extra_sem,
):
    xs, ys, cs = grid
    devices = slots_ref.shape[0]
    width, rows = text_ref.shape
    groups = img_ref.shape[1]
    old = devices * BS
    heads = keys.shape[0]
    longest = counts_ref[2 * devices] > 0
    load_extra = pltpu.make_async_copy(extra_hbm, extra, extra_sem)

    @pl.when(longest)
    def _():
        load_extra.start()

    diagonal = iota((groups, groups), 0) == iota((groups, groups), 1)
    mark = jnp.sum(jnp.where(diagonal, meta_ref[0:1], 0.0), axis=1, keepdims=True)
    row_of = (mark.astype(jnp.int32) - 1) * 4 + lax.rem(iota((groups, 1), 0), 4)
    hits = (iota((groups, rows), 1) == row_of).astype(F32)
    covered = jnp.sum(hits, axis=0, keepdims=True) > 0.0
    hits = hits.astype(BF16)
    squares = jnp.zeros((8, rows), F32)
    step = width // gain_ref.shape[0]
    for s in range(width // step):
        lines = slice(s * step, (s + 1) * step)
        placed = jnp.where(covered, dot(img_ref[lines], hits), text_ref[lines].astype(F32))
        squares = squares + jnp.sum((placed * placed).reshape(step // 8, 8, rows), axis=0)
        normed_ref[lines] = placed.astype(BF16)
    mean_square = jnp.sum(squares, axis=0, keepdims=True) / width
    scale = lax.rsqrt(mean_square + 1e-06)
    gains = jnp.transpose(gain_ref[...])
    for s in range(width // step):
        lines = slice(s * step, (s + 1) * step)
        normed_ref[lines] = (
            normed_ref[lines].astype(F32) * scale * gains[:, s : s + 1]
        ).astype(BF16)

    projected = dot(weight_ref[...], normed_ref[...])
    local = heads * HD
    cosine = cosine_ref[...]
    sine = sine_ref[...]

    def rotate(x):
        a = x[: HD // 2]
        b = x[HD // 2 :]
        return jnp.concatenate([a * cosine - b * sine, b * cosine + a * sine], axis=0)

    bias_lane = (iota((rows, 128 - HD), 1) == 0).astype(F32)
    queries = []
    for h in range(heads):
        query = rotate(projected[h * HD : (h + 1) * HD]).astype(BF16).astype(F32)
        query = jnp.transpose(query)
        queries.append(jnp.concatenate([query, bias_lane], axis=1).astype(BF16))
        key = rotate(projected[local + h * HD : local + (h + 1) * HD]).astype(BF16)
        value = projected[2 * local + h * HD : 2 * local + (h + 1) * HD].astype(BF16)
        cache_ref[0, h * HD : (h + 1) * HD] = key
        cache_ref[1, h * HD : (h + 1) * HD] = value
        keys[h, 0:HD, 0:rows] = key
        keys[h, HD:, 0:rows] = jnp.zeros((128 - HD, rows), BF16)
        values[h, :, 0:rows] = value

    lane = iota((128 - HD, 128), 1)
    top = iota((128 - HD, 128), 0) == 0

    def unpack(tile_of, count_of, column):
        tiles = [tile_of(w) for w in range(4)]
        limit = count_of(3)
        for w in (2, 1, 0):
            limit = jnp.where(lane < (w + 1) * BS, count_of(w), limit)
        bias = jnp.where(top & (lax.rem(lane, BS) >= limit), NEG, 0.0).astype(BF16)
        lanes = pl.ds(pl.multiple_of(column * 128, 128), 128)
        for h in range(heads):
            keys[h, 0:HD, lanes] = jnp.concatenate(
                [tile[:, h * BS : (h + 1) * BS] for tile in tiles], axis=1
            )
            keys[h, HD:, lanes] = bias
            at = (heads + h) * BS
            values[h, :, lanes] = jnp.concatenate(
                [tile[:, at : at + BS] for tile in tiles], axis=1
            )

    @pl.loop(0, devices // 4)
    def _(g):
        unpack(
            lambda w: slots_ref[g * 4 + w], lambda w: counts_ref[g * 4 + w], rows // 128 + g
        )

    @pl.when(longest)
    def _():
        load_extra.wait()

        @pl.loop(0, devices // 4)
        def _(g):
            def source(w):
                e = g * 4 + w
                c = e // (xs * ys)
                return lax.rem(e, xs * ys) * cs + c

            unpack(
                lambda w: extra[g * 4 + w],
                lambda w: counts_ref[devices + source(w)],
                rows // 128 + devices // 4 + g,
            )

    factor = HD ** (-0.5) * math.log2(math.e)
    half = min(256, rows)
    chunk = min(512, old)
    chunks = old // chunk + jnp.where(longest, old // chunk, 0)
    causal = iota((half, rows), 0) - iota((half, rows), 1)

    def fold(x, op):
        out = x[:, 0:128]
        for s in range(1, x.shape[1] // 128):
            out = op(out, x[:, s * 128 : (s + 1) * 128])
        return out

    for part in range(rows // half):
        q = [query[part * half : (part + 1) * half] for query in queries]
        tops = []
        for h in range(heads):
            own = dot(q[h], keys[h, :, 0:rows])
            own = jnp.where(causal >= -part * half, own, NEG)
            scores[h, :, 0:rows] = own
            tops.append(fold(own, jnp.maximum))

        def first_pass(n, tops):
            lanes = pl.ds(pl.multiple_of(rows + n * chunk, 128), chunk)
            out = []
            for h in range(heads):
                s = dot(q[h], keys[h, :, lanes])
                scores[h, :, lanes] = s
                out.append(jnp.maximum(tops[h], fold(s, jnp.maximum)))
            return out

        tops = lax.fori_loop(0, chunks, first_pass, tops)
        tops = [jnp.max(t, axis=1, keepdims=True) * factor for t in tops]

        def weigh(h, lanes):
            p = jnp.exp2(scores[h, :, lanes] * factor - tops[h])
            return dot(p.astype(BF16), values[h, :, lanes], 1, 1), fold(p, jnp.add)

        carry = []
        for h in range(heads):
            carry += list(weigh(h, slice(0, rows)))

        def second_pass(n, carry):
            lanes = pl.ds(pl.multiple_of(rows + n * chunk, 128), chunk)
            out = []
            for h in range(heads):
                mixed, total = weigh(h, lanes)
                out += [carry[2 * h] + mixed, carry[2 * h + 1] + total]
            return out

        carry = lax.fori_loop(0, chunks, second_pass, carry)
        for h in range(heads):
            mixed = carry[2 * h] / jnp.sum(carry[2 * h + 1], axis=1, keepdims=True)
            attended_ref[h * HD : (h + 1) * HD, part * half : (part + 1) * half] = jnp.transpose(
                mixed
            ).astype(BF16)


def attend(counts, text, img, meta, gain, weights, cosine, sine, slots, extra, grid):
    width, rows = text.shape
    local = weights.shape[0] // 3
    heads = local // HD
    devices = slots.shape[0]
    total = rows + 2 * devices * BS
    inside = pl.BlockSpec(memory_space=pltpu.VMEM)
    return pl.pallas_call(
        functools.partial(attend_kernel, grid),
        out_shape=(
            jax.ShapeDtypeStruct((local, rows), BF16),
            jax.ShapeDtypeStruct((2, local, rows), BF16),
        ),
        in_specs=[pl.BlockSpec(memory_space=pltpu.SMEM)]
        + [inside] * 8
        + [pl.BlockSpec(memory_space=pl.ANY)],
        out_specs=(inside, inside),
        scratch_shapes=[
            pltpu.VMEM(extra.shape, BF16),
            pltpu.VMEM((heads, 128, total), BF16),
            pltpu.VMEM((heads, HD, total), BF16),
            pltpu.VMEM((heads, min(256, rows), total), F32),
            pltpu.VMEM((width, rows), BF16),
            pltpu.SemaphoreType.DMA,
        ],
        compiler_params=pltpu.CompilerParams(vmem_limit_bytes=56 << 20),
        name="attend",
    )(counts, text, img, meta, gain, weights, cosine, sine, slots, extra)


def shards(
    vision, ln_gain, merge_proj, image_slot, text, rms_gain, wqkv, pcache, block_table, cache_len
):
    zs = lax.axis_size("head")
    devices = lax.axis_size("blk")
    here = lax.axis_index("blk")
    local, rows = text.shape
    width = local * zs
    owned = pcache.shape[2] // BS
    full_text = lax.all_gather(text, "head", axis=0, tiled=True)

    columns = block_table.shape[1]
    column = jnp.arange(columns, dtype=jnp.int32)[None, :]
    mine = (block_table >= 0) & (block_table // owned == here)
    key = column * owned + block_table % owned
    none = columns * owned
    first = jnp.min(jnp.where(mine, key, none), axis=1)
    twice = jnp.sum(mine.astype(jnp.int32), axis=1) > 1
    second = jnp.max(jnp.where(mine & twice[:, None], key, -1))
    indices = jnp.concatenate(
        [
            jnp.where(first < none, first % owned, 0),
            jnp.where(second >= 0, second % owned, 0)[None],
        ]
    )

    table_row = lax.dynamic_index_in_dim(block_table, here, 0, keepdims=True)
    held = (table_row >= 0) & (
        table_row // owned == jnp.arange(devices, dtype=jnp.int32)[:, None]
    )
    low = jnp.min(jnp.where(held, column, columns), axis=1)
    high = jnp.max(jnp.where(held, column, -1), axis=1)
    length = cache_len[0]
    valid = jnp.clip(length - low * BS, 0, BS)
    valid_second = jnp.where(high > low, jnp.clip(length - high * BS, 0, BS), 0)
    counts = jnp.concatenate([valid, valid_second, jnp.max(valid_second)[None]])

    half = HD // 2
    inverse = jnp.exp(jnp.arange(half, dtype=F32) * (-2.0 * math.log(10000.0) / HD))
    places = (length + jnp.arange(rows, dtype=jnp.int32)).astype(F32)
    angles = inverse[:, None] * places[None, :]
    cosine, sine = jnp.cos(angles), jnp.sin(angles)

    slots, extra, img, meta = communicate(
        width,
        rows,
        indices,
        image_slot.reshape(1, -1),
        ln_gain.reshape(1, local),
        vision,
        merge_proj.reshape(4 * local, width),
        pcache.reshape(4, HD, -1),
        devices,
        zs,
    )
    return attend(
        counts,
        full_text,
        img.reshape(width, -1),
        meta,
        rms_gain.reshape(zs, local),
        wqkv.reshape(3 * local, width),
        cosine,
        sine,
        slots,
        extra.reshape(slots.shape),
        GRID[devices],
    )


def solution(mesh):
    in_specs = (
        P(None, "head", "blk"),
        P("head"),
        P(None, "head", None),
        P("blk"),
        P("head", "blk"),
        P(),
        P(None, "head", None),
        P(None, "head", "blk"),
        P(),
        P("blk"),
    )
    out_specs = (P("head", "blk"), P(None, "head", "blk"))
    return jax.shard_map(shards, mesh=mesh, in_specs=in_specs, out_specs=out_specs, check_vma=False)
```
